32 devices in a mesh: dp: 8 (over y, x, core), rep: 4 (over z).
Axes of the slice: x: 2, y: 2, z: 4, core: 2. Of those that a mesh axis runs over, the one named last changes fastest.
Arguments:
- tokens: bfloat16 [4096, 2048], P(('dp', 'rep')), may hold values from -6 to 6
- cotangent: bfloat16 [4096, 2048], P(('dp', 'rep')), may hold values from -0.125 to 0.125
- doc_ids: int32 [64, 64], P(('dp', 'rep')), may hold values from 0 to 3, never falling along the last dimension, each value on 1 to 32 neighbouring positions
- valid_len: int32 [64], P(('dp', 'rep')), may hold values from 16 to 64
- w_qkv: bfloat16 [2048, 384], P('dp'), may hold values from -0.125 to 0.125
- w_out: bfloat16 [2048, 128], P('dp'), may hold values from -0.5 to 0.5
- norm_gain: bfloat16 [2048], P('dp'), may hold values from 0.5 to 1.5
Outputs:
- grad_qkv: float32 [2048, 384], P('dp')
- grad_out: float32 [2048, 128], P('dp')
- grad_gain: float32 [2048], P('dp')
The draws below stay inside these ranges and needn't reach their ends.
Inputs may be any that keep to these rules, and one draw needn't show every extreme that they name: `doc_ids`: within each row of 64 positions the ids never fall, and a document has 1 to 32 positions.
All inputs are finite; a program needn't handle non-finite values.
Results may differ from the reference program's by a relative error of at most 0.0079.
Values may be sent and summed in bfloat16 or wider, within the bound.
A program may use at most 64 MiB of HBM per device.

```python
import math
import jax
import jax.numpy as jnp
import numpy as np
from jax import lax

D = 2048
HD = 128
SEQ = 64
DOCS = 4
SAMPLES = 64
TOKENS = 4096
N_REP = 4


def touch_ends(entries, rng, least, largest):
    shape = entries.shape
    place = [jax.random.randint(jax.random.fold_in(rng, axis), (), 0, shape[axis]) for axis in range(len(shape))]
    entries = entries.at[tuple(place)].set(least)
    longest = shape.index(max(shape))
    place[longest] = (place[longest] + 1) % shape[longest]
    return entries.at[tuple(place)].set(largest)


def with_spikes(values, rng, source, target, blocks, factor):
    def block_of(dim):
        return (jnp.arange(values.shape[dim]) // (values.shape[dim] // blocks)).reshape((-1,) + (1,) * (values.ndim - 1 - dim))

    first = jax.random.permutation(rng, blocks)[block_of(target)]
    far = (block_of(target) + blocks // 2) % blocks
    return jnp.where((block_of(source) == first) | (block_of(source) == far), factor * values, values)


def shard_levels(stream_key, extent, split, low, top_value):
    def one(position, parts):
        heights = jax.random.uniform(jax.random.fold_in(jax.random.fold_in(stream_key, 6), position), (parts,), jnp.float32, low / len(split), top_value / len(split))
        return jnp.repeat(jnp.exp(heights), extent[position] // parts).reshape((-1,) + (1,) * (len(extent) - position - 1))

    factor_of = one(*split[0])
    for cut in split[1:]:
        factor_of = factor_of * one(*cut)
    return factor_of


def split_up(count, total, reach, skew):
    loads = [(1 << 20) // math.isqrt(standing ** skew) + 1 for standing in range(2, count + 1)]
    surplus, counts = total - reach - (count - 1), [1] * (count - 1)
    while surplus > 0:
        free = [i for i in range(count - 1) if counts[i] < reach]
        pool, remaining = sum([loads[i] for i in free]), surplus
        for i in free:
            addition = min(reach - counts[i], max(1, remaining * loads[i] // pool), surplus)
            counts[i] = counts[i] + addition
            surplus = surplus - addition
    return np.array([reach] + counts)


def ragged_sizes(key, count, total, reach, skew):
    if count == 2:
        one = jax.random.randint(key, (), max(1, total - reach), min(reach, total - 1) + 1)
        return jnp.stack([one, total - one])
    lengths = jnp.asarray(split_up(count, total, reach, skew), jnp.int32)
    twos = (count - 1) // 2
    donor, taker = lengths[1:1 + 2 * twos:2], lengths[2:2 + 2 * twos:2]
    room = jnp.minimum(donor - 1, reach - taker)
    moved = jax.random.randint(jax.random.fold_in(key, 1), (twos,), 0, 1 << 20) % (room + 1)
    lengths = lengths.at[1:1 + 2 * twos:2].set(donor - moved).at[2:2 + 2 * twos:2].set(taker + moved)
    return lengths[jax.random.permutation(jax.random.fold_in(key, 2), count)]


def centred(rng, dims, deviation, most, split=(), kind=jnp.bfloat16):
    level = shard_levels(rng, dims, split, -0.22, 0.18) if split else 1.0
    array = jax.random.normal(rng, dims, jnp.float32) * deviation * level
    return jnp.minimum(jnp.maximum(array, -most), most).astype(kind)


def gaussian_with(own_key, shape, width, most, pieces, heavy, kind=jnp.bfloat16):
    values = width * jax.random.normal(own_key, shape, jnp.float32)
    if pieces:
        values = values * shard_levels(own_key, shape, pieces, -0.22, 0.18)
    return jnp.clip(with_spikes(values, jax.random.fold_in(own_key, 3), *heavy), -most, most).astype(kind)


def setup_inputs(seed: int = 0) -> dict:
    arg_keys = jax.random.split(jax.random.key(seed), 8)
    return {
        "tokens": gaussian_with(arg_keys[0], (TOKENS, D), 1.0, 6.0, ((0, 32),), (0, 1, 32, 2.75)),
        "cotangent": gaussian_with(arg_keys[1], (TOKENS, D), 0.01, 0.125, ((0, 32),), (0, 1, 32, 2.75)),
        "doc_ids": jax.vmap(lambda own: jnp.searchsorted(jnp.cumsum(ragged_sizes(own, DOCS, SEQ, SEQ // 2, 0)), jnp.arange(SEQ), side="right"))(jax.random.split(arg_keys[2], SAMPLES)).reshape((SAMPLES, SEQ)).astype(jnp.int32),
        "valid_len": touch_ends(jax.random.randint(arg_keys[3], (SAMPLES,), SEQ // 4, SEQ + 1), jax.random.fold_in(arg_keys[3], 1), SEQ // 4, SEQ).astype(jnp.int32),
        "w_qkv": centred(arg_keys[4], (D, 3 * HD), D ** -0.5, 0.125, ((0, 8),)),
        "w_out": centred(arg_keys[5], (D, HD), HD ** -0.5, 0.5, ((0, 8),)),
        "norm_gain": jnp.clip(1.0 + 0.1 * jax.random.normal(arg_keys[6], (D,), jnp.float32), 0.5, 1.5).astype(jnp.bfloat16),
    }


NORM_EPS = 1e-06
ROPE_BASE = 1000000.0

def rotate(vector):
    half_size = vector.shape[-1] // 2
    return jnp.concatenate([-vector[..., half_size:], vector[..., :half_size]], axis=-1)

def unrotate(vector):
    half_size = vector.shape[-1] // 2
    return jnp.concatenate([vector[..., half_size:], -vector[..., :half_size]], axis=-1)

def tables(doc_rows, head_size):
    seq_length = doc_rows.shape[1]
    earlier = lax.optimization_barrier(jnp.sum((doc_rows[:, None, :] < doc_rows[:, :, None]).astype(jnp.int32), axis=2))
    offsets = (jnp.arange(seq_length, dtype=jnp.int32)[None, :] - earlier).astype(jnp.float32)
    frequency = ROPE_BASE ** (-2.0 * jnp.arange(head_size // 2, dtype=jnp.float32) / head_size)
    angles = offsets[:, :, None] * frequency
    angles = jnp.concatenate([angles, angles], axis=2)
    return (jnp.cos(angles), jnp.sin(angles))

def reference(tokens, cotangent, doc_ids, valid_len, w_qkv, w_out, norm_gain):
    samples, seq_length = doc_ids.shape
    model_width = tokens.shape[1]
    inputs = tokens.reshape(samples, seq_length, model_width)
    grads_in = cotangent.reshape(samples, seq_length, model_width)
    scale = 1.0 / math.sqrt(HD)
    order_row = jnp.arange(seq_length, dtype=jnp.int32)[:, None]
    order_col = jnp.arange(seq_length, dtype=jnp.int32)[None, :]

    def step(totals, item):
        x_rows, dy_rows, doc_row, valid = item
        wide_in = x_rows.astype(jnp.float32)
        inverse_rms = lax.rsqrt(lax.optimization_barrier(jnp.mean(wide_in * wide_in, axis=1, keepdims=True)) + NORM_EPS)
        scaled_in = wide_in * inverse_rms
        normed = (scaled_in * norm_gain.astype(jnp.float32)).astype(jnp.bfloat16)
        projected = jnp.dot(normed, w_qkv, preferred_element_type=jnp.float32)
        cosine, sine_part = tables(doc_row[None, :], HD)
        cosine = cosine[0]
        sine_part = sine_part[0]
        queries = projected[:, :HD]
        keys_raw = projected[:, HD:2 * HD]
        values_raw = projected[:, 2 * HD:]
        query_rot = ((queries * cosine + rotate(queries) * sine_part) * scale).astype(jnp.bfloat16)
        key_rot = (keys_raw * cosine + rotate(keys_raw) * sine_part).astype(jnp.bfloat16)
        values = values_raw.astype(jnp.bfloat16)
        scores = jnp.dot(query_rot, key_rot.T, preferred_element_type=jnp.float32)
        allowed = (doc_row[:, None] == doc_row[None, :]) & (order_col <= order_row)
        raised = jnp.where(allowed, jnp.exp(scores), 0.0)
        probabilities = raised / lax.optimization_barrier(jnp.sum(raised, axis=1, keepdims=True))
        probs_low = probabilities.astype(jnp.bfloat16)
        attended = jnp.dot(probs_low, values, preferred_element_type=jnp.float32).astype(jnp.bfloat16)
        live_rows = jnp.arange(seq_length, dtype=jnp.int32) < valid
        live_dy = jnp.where(live_rows[:, None], dy_rows, jnp.zeros((), jnp.bfloat16))
        d_attended = jnp.dot(live_dy, w_out, preferred_element_type=jnp.float32).astype(jnp.bfloat16)
        d_probs = jnp.dot(d_attended, values.T, preferred_element_type=jnp.float32)
        d_values = jnp.dot(probs_low.T, d_attended, preferred_element_type=jnp.float32)
        d_scores = (probabilities * (d_probs - lax.optimization_barrier(jnp.sum(probabilities * d_probs, axis=1, keepdims=True)))).astype(jnp.bfloat16)
        d_query = jnp.dot(d_scores, key_rot, preferred_element_type=jnp.float32) * scale
        d_key = jnp.dot(d_scores.T, query_rot, preferred_element_type=jnp.float32)
        d_query = d_query * cosine + unrotate(d_query * sine_part)
        d_key = d_key * cosine + unrotate(d_key * sine_part)
        d_qkv = jnp.concatenate([d_query, d_key, d_values], axis=1).astype(jnp.bfloat16)
        d_normed = jnp.dot(d_qkv, w_qkv.T, preferred_element_type=jnp.float32)
        gain_term = lax.optimization_barrier(jnp.sum(d_normed * scaled_in, axis=0))
        new_totals = (totals[0] + jnp.dot(normed.T, d_qkv, preferred_element_type=jnp.float32), totals[1] + jnp.dot(live_dy.T, attended, preferred_element_type=jnp.float32), totals[2] + gain_term)
        return (new_totals, None)
    initial = (jnp.zeros((model_width, 3 * HD), jnp.float32), jnp.zeros((model_width, HD), jnp.float32), jnp.zeros((model_width,), jnp.float32))
    totals, _ = lax.scan(step, initial, (inputs, grads_in, doc_ids, valid_len))
    return (totals[0] / N_REP, totals[1] / N_REP, totals[2] / N_REP)
```

```python
import functools
import math

import jax
import jax.numpy as jnp
from jax import lax
from jax.experimental import pallas as pl
from jax.experimental.pallas import tpu as pltpu
from jax.sharding import PartitionSpec as P

NORM_EPS = 1e-06
ROPE_BASE = 1000000.0


def rotate(vector):
    half_size = vector.shape[-1] // 2
    return jnp.concatenate([-vector[..., half_size:], vector[..., :half_size]], axis=-1)


def unrotate(vector):
    half_size = vector.shape[-1] // 2
    return jnp.concatenate([vector[..., half_size:], -vector[..., :half_size]], axis=-1)


def tables(doc_rows, head_size):
    seq_length = doc_rows.shape[1]
    earlier = jnp.sum((doc_rows[:, None, :] < doc_rows[:, :, None]).astype(jnp.int32), axis=2)
    offsets = (jnp.arange(seq_length, dtype=jnp.int32)[None, :] - earlier).astype(jnp.float32)
    frequency = ROPE_BASE ** (-2.0 * jnp.arange(head_size // 2, dtype=jnp.float32) / head_size)
    angles = offsets[:, :, None] * frequency
    angles = jnp.concatenate([angles, angles], axis=2)
    return (jnp.cos(angles), jnp.sin(angles))


def forward_pass(inputs, doc_rows, w_qkv_full, gain_full):
    batches, seq_length, model_width = inputs.shape
    head_size = w_qkv_full.shape[1] // 3
    scale = 1.0 / math.sqrt(head_size)
    wide_in = inputs.astype(jnp.float32)
    inverse_rms = lax.rsqrt(jnp.mean(wide_in * wide_in, axis=2, keepdims=True) + NORM_EPS)
    scaled_in = wide_in * inverse_rms
    normed = (scaled_in * gain_full.astype(jnp.float32)).astype(jnp.bfloat16)
    projected = jnp.dot(
        normed.reshape(-1, model_width), w_qkv_full, preferred_element_type=jnp.float32
    )
    projected = projected.reshape(batches, seq_length, 3 * head_size)
    cosine, sine_part = tables(doc_rows, head_size)
    queries = projected[:, :, :head_size]
    keys_raw = projected[:, :, head_size : 2 * head_size]
    values_raw = projected[:, :, 2 * head_size :]
    query_rot = ((queries * cosine + rotate(queries) * sine_part) * scale).astype(jnp.bfloat16)
    key_rot = (keys_raw * cosine + rotate(keys_raw) * sine_part).astype(jnp.bfloat16)
    values = values_raw.astype(jnp.bfloat16)
    scores = jnp.einsum("msh,mth->mst", query_rot, key_rot, preferred_element_type=jnp.float32)
    order_row = jnp.arange(seq_length, dtype=jnp.int32)[:, None]
    order_col = jnp.arange(seq_length, dtype=jnp.int32)[None, :]
    allowed = (doc_rows[:, :, None] == doc_rows[:, None, :]) & (order_col <= order_row)[None]
    raised = jnp.where(allowed, jnp.exp(scores), 0.0)
    probabilities = raised / jnp.sum(raised, axis=2, keepdims=True)
    probs_low = probabilities.astype(jnp.bfloat16)
    attended = jnp.einsum(
        "mst,mth->msh", probs_low, values, preferred_element_type=jnp.float32
    ).astype(jnp.bfloat16)
    return (
        scaled_in,
        normed,
        query_rot,
        key_rot,
        values,
        probabilities,
        probs_low,
        attended,
        cosine,
        sine_part,
    )


def backward_pass(saved, live_dy, w_qkv_full, w_out_full):
    (
        scaled_in,
        normed,
        query_rot,
        key_rot,
        values,
        probabilities,
        probs_low,
        attended,
        cosine,
        sine_part,
    ) = saved
    batches, seq_length, model_width = live_dy.shape
    head_size = w_out_full.shape[1]
    scale = 1.0 / math.sqrt(head_size)
    d_attended = jnp.dot(
        live_dy.reshape(-1, model_width), w_out_full, preferred_element_type=jnp.float32
    )
    d_attended = d_attended.reshape(batches, seq_length, head_size).astype(jnp.bfloat16)
    d_probs = jnp.einsum("msh,mth->mst", d_attended, values, preferred_element_type=jnp.float32)
    d_values = jnp.einsum("mst,msh->mth", probs_low, d_attended, preferred_element_type=jnp.float32)
    d_scores = (
        probabilities * (d_probs - jnp.sum(probabilities * d_probs, axis=2, keepdims=True))
    ).astype(jnp.bfloat16)
    d_query = (
        jnp.einsum("mst,mth->msh", d_scores, key_rot, preferred_element_type=jnp.float32) * scale
    )
    d_key = jnp.einsum("mst,msh->mth", d_scores, query_rot, preferred_element_type=jnp.float32)
    d_query = d_query * cosine + unrotate(d_query * sine_part)
    d_key = d_key * cosine + unrotate(d_key * sine_part)
    d_qkv = jnp.concatenate([d_query, d_key, d_values], axis=2).astype(jnp.bfloat16)
    d_normed = lax.dot_general(
        d_qkv.reshape(-1, 3 * head_size),
        w_qkv_full,
        (((1,), (1,)), ((), ())),
        preferred_element_type=jnp.float32,
    )
    gain_term = jnp.sum(d_normed * scaled_in.reshape(-1, model_width), axis=0)
    return (d_qkv, gain_term)


def shards(tokens, cotangent, doc_ids, valid_len, w_qkv, w_out, norm_gain):
    batches, seq_length = doc_ids.shape
    model_width = tokens.shape[1]
    inputs = tokens.reshape(batches, seq_length, model_width)
    live_rows = jnp.arange(seq_length, dtype=jnp.int32)[None, :] < valid_len[:, None]
    live_dy = jnp.where(
        live_rows[:, :, None],
        cotangent.reshape(batches, seq_length, model_width),
        jnp.zeros((), jnp.bfloat16),
    )
    full_set = (
        lax.all_gather(w_qkv, "dp", axis=0, tiled=True),
        lax.all_gather(w_out, "dp", axis=0, tiled=True),
        lax.all_gather(norm_gain, "dp", axis=0, tiled=True),
    )
    saved = forward_pass(inputs, doc_ids, full_set[0], full_set[2])
    qkv_all, gain_total = backward_pass(saved, live_dy, full_set[0], full_set[1])
    normed_all = saved[1]
    attended_all = saved[7]
    head_size = w_out.shape[1]
    normed_flat = normed_all.reshape(-1, model_width)
    qkv_flat = qkv_all.reshape(-1, 3 * head_size)
    attended_flat = attended_all.reshape(-1, head_size)
    grad_qkv = lax.dot_general(
        normed_flat, qkv_flat, (((0,), (0,)), ((), ())), preferred_element_type=jnp.float32
    )
    grad_out = lax.dot_general(
        live_dy.reshape(-1, model_width),
        attended_flat,
        (((0,), (0,)), ((), ())),
        preferred_element_type=jnp.float32,
    )
    shares = (
        lax.psum_scatter(grad_qkv, "dp", scatter_dimension=0, tiled=True),
        lax.psum_scatter(grad_out, "dp", scatter_dimension=0, tiled=True),
    )
    shares = lax.psum((shares[0], shares[1]), "rep")
    gain_whole = lax.psum(gain_total, ("dp", "rep"))
    owned_rows = w_qkv.shape[0]
    gain_start = lax.axis_index("dp") * owned_rows
    gain_owned = lax.dynamic_slice_in_dim(gain_whole, gain_start, owned_rows, 0)
    replicas = lax.axis_size("rep")
    return (shares[0] / replicas, shares[1] / replicas, gain_owned / replicas)


MESH = pl.DeviceIdType.MESH
LANES = 128
CORES = 2


def mm(left, right, dims):
    return lax.dot_general(left, right, (dims, ((), ())), preferred_element_type=jnp.float32)


def eye(size):
    return lax.broadcasted_iota(jnp.int32, (size, size), 0) == lax.broadcasted_iota(
        jnp.int32, (size, size), 1
    )


def to_column(row):
    return jnp.sum(jnp.where(eye(row.shape[1]), row, 0.0), axis=1, keepdims=True)


def to_row(column):
    return jnp.sum(jnp.where(eye(column.shape[0]), column, 0.0), axis=0, keepdims=True)


def fused(
    n,
    replicas,
    x_ref,
    dy_ref,
    doc_ref,
    valid_ref,
    wq_ref,
    wo_ref,
    gain_ref,
    gq_ref,
    go_ref,
    gg_ref,
    w_all,
    x_all,
    dy_all,
    y_all,
    acc,
    rs_send,
    rs_recv,
    g_all,
    w_send_sem,
    w_recv_sem,
    a_send_sem,
    a_recv_sem,
    y_send_sem,
    y_recv_sem,
    r_send_sem,
    r_recv_sem,
    g_send_sem,
    g_recv_sem,
):
    me = lax.axis_index("dp")
    rep = lax.axis_index("rep")
    chips = n // CORES
    chip, core = me // CORES, lax.rem(me, CORES)
    sibling = chip * CORES + (1 - core)
    rows, width = x_ref.shape
    owned = wq_ref.shape[0]
    head = wo_ref.shape[1]
    wide = 3 * head
    samples, seq = doc_ref.shape
    piece = owned // replicas
    scale = 1.0 / math.sqrt(head)

    barrier = pltpu.get_barrier_semaphore()
    for off in range(1, n):
        pl.semaphore_signal(
            barrier, inc=1, device_id={"dp": lax.rem(me + off, n)}, device_id_type=MESH
        )
    for off in range(1, replicas):
        pl.semaphore_signal(
            barrier,
            inc=1,
            device_id={"rep": lax.rem(rep + off, replicas)},
            device_id_type=MESH,
        )

    gain_col = to_column(gain_ref[...].astype(jnp.float32))
    my_w = pl.ds(pl.multiple_of(me * owned, LANES), owned)
    w_all[my_w, :wide] = (wq_ref[...].astype(jnp.float32) * gain_col).astype(jnp.bfloat16)
    w_all[my_w, wide:] = wo_ref[...]

    pl.semaphore_wait(barrier, n - 1 + replicas - 1)

    pending = []

    def send(src, dst, send_sem, recv_sem, where):
        copy = pltpu.make_async_remote_copy(
            src_ref=src,
            dst_ref=dst,
            send_sem=send_sem,
            recv_sem=recv_sem,
            device_id=where,
            device_id_type=MESH,
        )
        copy.start()
        pending.append(copy)
        return copy

    def origin(off, other):
        lane = 1 - core if other else core
        return lax.rem(chip + chips - off, chips) * CORES + lane

    def spread(buf, block, send_sem, recv_sem):
        mine = buf.at[pl.ds(pl.multiple_of(me * block, LANES), block)]
        direct = {}
        for off in range(1, chips):
            peer = lax.rem(chip + off, chips) * CORES + core
            direct[off] = send(mine, mine, send_sem.at[off], recv_sem.at[off], {"dp": peer})
        passed = {
            0: send(mine, mine, send_sem.at[chips], recv_sem.at[chips], {"dp": sibling})
        }
        return direct, passed

    def hand_on(buf, block, off, direct, passed, send_sem, recv_sem):
        direct[off].wait_recv()
        got = buf.at[pl.ds(pl.multiple_of(origin(off, False) * block, LANES), block)]
        passed[off] = send(
            got, got, send_sem.at[chips + off], recv_sem.at[chips + off], {"dp": sibling}
        )

    direct, passed = spread(w_all, owned, w_send_sem, w_recv_sem)

    wide_in = x_ref[...].astype(jnp.float32)
    inverse = lax.rsqrt(
        jnp.sum(wide_in * wide_in, axis=1, keepdims=True) * (1.0 / width) + NORM_EPS
    )
    keys, live = [], []
    for m in range(samples):
        doc_row = doc_ref[m : m + 1, :].astype(jnp.float32)
        keys.append(to_column(doc_row) + float(m * seq))
        place = lax.broadcasted_iota(jnp.int32, (seq, 1), 0)
        live.append(jnp.where(place < valid_ref[m], 1.0, 0.0))
    key_col = jnp.concatenate(keys, axis=0)
    live_col = jnp.concatenate(live, axis=0)
    key_row = to_row(key_col)
    earlier = jnp.sum(jnp.where(key_row < key_col, 1.0, 0.0), axis=1, keepdims=True)
    order_row = lax.broadcasted_iota(jnp.int32, (rows, rows), 0)
    order_col = lax.broadcasted_iota(jnp.int32, (rows, rows), 1)
    allowed = (key_row == key_col) & (order_col <= order_row)
    offsets = lax.broadcasted_iota(jnp.int32, (rows, 1), 0).astype(jnp.float32) - earlier
    lane = lax.broadcasted_iota(jnp.int32, (1, head), 1)
    half = lax.rem(lane, head // 2).astype(jnp.float32)
    frequency = jnp.exp(half * (-2.0 / head * math.log(ROPE_BASE)))
    angles = offsets * frequency
    cosine = jnp.cos(angles)
    signed = jnp.sin(angles) * jnp.where(lane < head // 2, -1.0, 1.0)

    def times(source, total):
        cols = pl.ds(pl.multiple_of(source * owned, LANES), owned)
        projected = mm(x_ref[:, cols], w_all[cols, :wide], ((1,), (0,)))
        d_att = mm(dy_ref[:, cols], w_all[cols, wide:], ((1,), (0,)))
        if total is None:
            return projected, d_att
        return total[0] + projected, total[1] + d_att

    total = times(me, None)
    passed[0].wait_recv()
    total = times(sibling, total)
    for off in range(1, chips):
        hand_on(w_all, owned, off, direct, passed, w_send_sem, w_recv_sem)
        total = times(origin(off, False), total)

    my_rows = pl.ds(pl.multiple_of(me * rows, LANES), rows)
    columns = {}
    for off in range(1, n):
        peer = lax.rem(me + off, n)
        cols = pl.ds(pl.multiple_of(peer * owned, LANES), owned)
        columns[off] = (
            send(
                x_ref.at[:, cols],
                x_all.at[my_rows],
                a_send_sem.at[0, off],
                a_recv_sem.at[0, off],
                {"dp": peer},
            ),
            send(
                dy_ref.at[:, cols],
                dy_all.at[my_rows],
                a_send_sem.at[1, off],
                a_recv_sem.at[1, off],
                {"dp": peer},
            ),
        )

    for off in range(1, chips):
        passed[off].wait_recv()
        total = times(origin(off, True), total)

    projected = total[0] * inverse
    d_att = (total[1] * live_col).astype(jnp.bfloat16)

    def turn(vector, sine_part):
        return vector * cosine + pltpu.roll(vector, head // 2, 1) * sine_part

    query = (turn(projected[:, :head], signed) * scale).astype(jnp.bfloat16)
    key = turn(projected[:, head : 2 * head], signed).astype(jnp.bfloat16)
    values = projected[:, 2 * head :].astype(jnp.bfloat16)
    scores = mm(query, key, ((1,), (1,)))
    raised = jnp.where(allowed, jnp.exp(scores), 0.0)
    probs = raised / jnp.sum(raised, axis=1, keepdims=True)
    probs_low = probs.astype(jnp.bfloat16)
    attended = mm(probs_low, values, ((1,), (0,)))
    d_probs = mm(d_att, values, ((1,), (1,)))
    d_values = mm(probs_low, d_att, ((0,), (0,)))
    d_scores = (
        probs * (d_probs - jnp.sum(probs * d_probs, axis=1, keepdims=True))
    ).astype(jnp.bfloat16)
    d_query = turn(mm(d_scores, key, ((1,), (0,))) * scale, -signed)
    d_key = turn(mm(d_scores, query, ((0,), (0,))), -signed)
    y_all[my_rows, :head] = (d_query * inverse).astype(jnp.bfloat16)
    y_all[my_rows, head : 2 * head] = (d_key * inverse).astype(jnp.bfloat16)
    y_all[my_rows, 2 * head : wide] = (d_values * inverse).astype(jnp.bfloat16)
    y_all[my_rows, wide:] = (attended * live_col).astype(jnp.bfloat16)

    direct, passed = spread(y_all, rows, y_send_sem, y_recv_sem)

    my_cols = pl.ds(pl.multiple_of(me * owned, LANES), owned)
    acc[:, :wide] = mm(x_ref[:, my_cols], y_all[my_rows, :wide], ((0,), (0,)))
    acc[:, wide:] = mm(dy_ref[:, my_cols], y_all[my_rows, wide:], ((0,), (0,)))
    for off in range(1, n):
        for copy in columns[off]:
            copy.wait_recv()

    def gather(source):
        part = pl.ds(pl.multiple_of(source * rows, LANES), rows)
        acc[:, :wide] += mm(x_all[part, :], y_all[part, :wide], ((0,), (0,)))
        acc[:, wide:] += mm(dy_all[part, :], y_all[part, wide:], ((0,), (0,)))

    passed[0].wait_recv()
    gather(sibling)
    for off in range(1, chips):
        hand_on(y_all, rows, off, direct, passed, y_send_sem, y_recv_sem)
        gather(origin(off, False))
    for off in range(1, chips):
        passed[off].wait_recv()
        gather(origin(off, True))

    rs_send[...] = acc[...].astype(jnp.bfloat16)
    sums = []
    for off in range(1, replicas):
        peer = lax.rem(rep + off, replicas)
        part = pl.ds(pl.multiple_of(peer * piece, 16), piece)
        sums.append(
            send(
                rs_send.at[part],
                rs_recv.at[off - 1],
                r_send_sem.at[off],
                r_recv_sem.at[off],
                {"rep": peer},
            )
        )
    mine = pl.ds(pl.multiple_of(rep * piece, 16), piece)
    whole = acc[mine, :]
    for off in range(1, replicas):
        sums[off - 1].wait_recv()
        whole = whole + rs_recv[off - 1].astype(jnp.float32)
    g_all[mine, :] = (whole * (1.0 / replicas)).astype(jnp.bfloat16)
    last = []
    for off in range(1, replicas):
        peer = lax.rem(rep + off, replicas)
        last.append(
            send(
                g_all.at[mine],
                g_all.at[mine],
                g_send_sem.at[off],
                g_recv_sem.at[off],
                {"rep": peer},
            )
        )
    for copy in last:
        copy.wait_recv()
    total_q = g_all[:, :wide].astype(jnp.float32)
    gq_ref[...] = total_q * gain_col
    go_ref[...] = g_all[:, wide:].astype(jnp.float32)
    gg_ref[...] = to_row(
        jnp.sum(total_q * wq_ref[...].astype(jnp.float32), axis=1, keepdims=True)
    )
    for copy in pending:
        copy.wait_send()


def one_kernel(n, replicas, tokens, cotangent, doc_ids, valid_len, w_qkv, w_out, norm_gain):
    rows, width = tokens.shape
    owned, wide = w_qkv.shape
    head = w_out.shape[1]
    chips = n // CORES
    vmem = pl.BlockSpec(memory_space=pltpu.VMEM)
    smem = pl.BlockSpec(memory_space=pltpu.SMEM)
    low = jnp.bfloat16
    full = wide + head
    sem = pltpu.SemaphoreType.DMA
    grad_qkv, grad_out, grad_gain = pl.pallas_call(
        functools.partial(fused, n, replicas),
        out_shape=(
            jax.ShapeDtypeStruct((owned, wide), jnp.float32),
            jax.ShapeDtypeStruct((owned, head), jnp.float32),
            jax.ShapeDtypeStruct((1, owned), jnp.float32),
        ),
        in_specs=[vmem, vmem, vmem, smem, vmem, vmem, vmem],
        out_specs=(vmem, vmem, vmem),
        scratch_shapes=[
            pltpu.VMEM((width, full), low),
            pltpu.VMEM((n * rows, owned), low),
            pltpu.VMEM((n * rows, owned), low),
            pltpu.VMEM((n * rows, full), low),
            pltpu.VMEM((owned, full), jnp.float32),
            pltpu.VMEM((owned, full), low),
            pltpu.VMEM((replicas - 1, owned // replicas, full), low),
            pltpu.VMEM((owned, full), low),
            sem((2 * chips,)),
            sem((2 * chips,)),
            sem((2, n)),
            sem((2, n)),
            sem((2 * chips,)),
            sem((2 * chips,)),
            sem((replicas,)),
            sem((replicas,)),
            sem((replicas,)),
            sem((replicas,)),
        ],
        compiler_params=pltpu.CompilerParams(
            collective_id=0, has_side_effects=True, vmem_limit_bytes=48 * 1024 * 1024
        ),
    )(tokens, cotangent, doc_ids, valid_len, w_qkv, w_out, norm_gain.reshape(1, owned))
    return grad_qkv, grad_out, grad_gain.reshape(owned)


def shards_or_kernel(
    n, replicas, tokens, cotangent, doc_ids, valid_len, w_qkv, w_out, norm_gain
):
    rows, owned, head = tokens.shape[0], w_qkv.shape[0], w_out.shape[1]
    fits = (
        n % CORES == 0
        and n > CORES
        and replicas > 1
        and owned % LANES == 0
        and owned % (16 * replicas) == 0
        and rows % LANES == 0
        and rows * n <= 2048
        and head == LANES
        and doc_ids.shape[1] % 8 == 0
    )
    if not fits:
        return shards(tokens, cotangent, doc_ids, valid_len, w_qkv, w_out, norm_gain)
    return one_kernel(
        n, replicas, tokens, cotangent, doc_ids, valid_len, w_qkv, w_out, norm_gain
    )


def solution(mesh):
    in_specs = (
        P(("dp", "rep"), None),
        P(("dp", "rep"), None),
        P(("dp", "rep"), None),
        P(("dp", "rep")),
        P("dp", None),
        P("dp", None),
        P("dp"),
    )
    out_specs = (P("dp", None), P("dp", None), P("dp"))
    body = functools.partial(shards_or_kernel, mesh.shape["dp"], mesh.shape["rep"])
    return jax.shard_map(body, mesh=mesh, in_specs=in_specs, out_specs=out_specs, check_vma=False)
```

```python
import functools
import itertools
import math

import jax
import jax.numpy as jnp
from jax import lax
from jax.experimental import pallas as pl
from jax.experimental.pallas import tpu as pltpu
from jax.sharding import PartitionSpec as P

NORM_EPS = 1e-06
ROPE_BASE = 1000000.0


def rotate(vector):
    half_size = vector.shape[-1] // 2
    return jnp.concatenate([-vector[..., half_size:], vector[..., :half_size]], axis=-1)


def unrotate(vector):
    half_size = vector.shape[-1] // 2
    return jnp.concatenate([vector[..., half_size:], -vector[..., :half_size]], axis=-1)


def tables(doc_rows, head_size):
    seq_length = doc_rows.shape[1]
    earlier = jnp.sum((doc_rows[:, None, :] < doc_rows[:, :, None]).astype(jnp.int32), axis=2)
    offsets = (jnp.arange(seq_length, dtype=jnp.int32)[None, :] - earlier).astype(jnp.float32)
    frequency = ROPE_BASE ** (-2.0 * jnp.arange(head_size // 2, dtype=jnp.float32) / head_size)
    angles = offsets[:, :, None] * frequency
    angles = jnp.concatenate([angles, angles], axis=2)
    return (jnp.cos(angles), jnp.sin(angles))


def forward_pass(inputs, doc_rows, w_qkv_full, gain_full):
    batches, seq_length, model_width = inputs.shape
    head_size = w_qkv_full.shape[1] // 3
    scale = 1.0 / math.sqrt(head_size)
    wide_in = inputs.astype(jnp.float32)
    inverse_rms = lax.rsqrt(jnp.mean(wide_in * wide_in, axis=2, keepdims=True) + NORM_EPS)
    scaled_in = wide_in * inverse_rms
    normed = (scaled_in * gain_full.astype(jnp.float32)).astype(jnp.bfloat16)
    projected = jnp.dot(
        normed.reshape(-1, model_width), w_qkv_full, preferred_element_type=jnp.float32
    )
    projected = projected.reshape(batches, seq_length, 3 * head_size)
    cosine, sine_part = tables(doc_rows, head_size)
    queries = projected[:, :, :head_size]
    keys_raw = projected[:, :, head_size : 2 * head_size]
    values_raw = projected[:, :, 2 * head_size :]
    query_rot = ((queries * cosine + rotate(queries) * sine_part) * scale).astype(jnp.bfloat16)
    key_rot = (keys_raw * cosine + rotate(keys_raw) * sine_part).astype(jnp.bfloat16)
    values = values_raw.astype(jnp.bfloat16)
    scores = jnp.einsum("msh,mth->mst", query_rot, key_rot, preferred_element_type=jnp.float32)
    order_row = jnp.arange(seq_length, dtype=jnp.int32)[:, None]
    order_col = jnp.arange(seq_length, dtype=jnp.int32)[None, :]
    allowed = (doc_rows[:, :, None] == doc_rows[:, None, :]) & (order_col <= order_row)[None]
    raised = jnp.where(allowed, jnp.exp(scores), 0.0)
    probabilities = raised / jnp.sum(raised, axis=2, keepdims=True)
    probs_low = probabilities.astype(jnp.bfloat16)
    attended = jnp.einsum(
        "mst,mth->msh", probs_low, values, preferred_element_type=jnp.float32
    ).astype(jnp.bfloat16)
    return (
        scaled_in,
        normed,
        query_rot,
        key_rot,
        values,
        probabilities,
        probs_low,
        attended,
        cosine,
        sine_part,
    )


def backward_pass(saved, live_dy, w_qkv_full, w_out_full):
    (
        scaled_in,
        normed,
        query_rot,
        key_rot,
        values,
        probabilities,
        probs_low,
        attended,
        cosine,
        sine_part,
    ) = saved
    batches, seq_length, model_width = live_dy.shape
    head_size = w_out_full.shape[1]
    scale = 1.0 / math.sqrt(head_size)
    d_attended = jnp.dot(
        live_dy.reshape(-1, model_width), w_out_full, preferred_element_type=jnp.float32
    )
    d_attended = d_attended.reshape(batches, seq_length, head_size).astype(jnp.bfloat16)
    d_probs = jnp.einsum("msh,mth->mst", d_attended, values, preferred_element_type=jnp.float32)
    d_values = jnp.einsum("mst,msh->mth", probs_low, d_attended, preferred_element_type=jnp.float32)
    d_scores = (
        probabilities * (d_probs - jnp.sum(probabilities * d_probs, axis=2, keepdims=True))
    ).astype(jnp.bfloat16)
    d_query = (
        jnp.einsum("mst,mth->msh", d_scores, key_rot, preferred_element_type=jnp.float32) * scale
    )
    d_key = jnp.einsum("mst,msh->mth", d_scores, query_rot, preferred_element_type=jnp.float32)
    d_query = d_query * cosine + unrotate(d_query * sine_part)
    d_key = d_key * cosine + unrotate(d_key * sine_part)
    d_qkv = jnp.concatenate([d_query, d_key, d_values], axis=2).astype(jnp.bfloat16)
    d_normed = lax.dot_general(
        d_qkv.reshape(-1, 3 * head_size),
        w_qkv_full,
        (((1,), (1,)), ((), ())),
        preferred_element_type=jnp.float32,
    )
    gain_term = jnp.sum(d_normed * scaled_in.reshape(-1, model_width), axis=0)
    return (d_qkv, gain_term)


def shards(tokens, cotangent, doc_ids, valid_len, w_qkv, w_out, norm_gain):
    batches, seq_length = doc_ids.shape
    model_width = tokens.shape[1]
    inputs = tokens.reshape(batches, seq_length, model_width)
    live_rows = jnp.arange(seq_length, dtype=jnp.int32)[None, :] < valid_len[:, None]
    live_dy = jnp.where(
        live_rows[:, :, None],
        cotangent.reshape(batches, seq_length, model_width),
        jnp.zeros((), jnp.bfloat16),
    )
    full_set = (
        lax.all_gather(w_qkv, "dp", axis=0, tiled=True),
        lax.all_gather(w_out, "dp", axis=0, tiled=True),
        lax.all_gather(norm_gain, "dp", axis=0, tiled=True),
    )
    saved = forward_pass(inputs, doc_ids, full_set[0], full_set[2])
    qkv_all, gain_total = backward_pass(saved, live_dy, full_set[0], full_set[1])
    normed_all = saved[1]
    attended_all = saved[7]
    head_size = w_out.shape[1]
    normed_flat = normed_all.reshape(-1, model_width)
    qkv_flat = qkv_all.reshape(-1, 3 * head_size)
    attended_flat = attended_all.reshape(-1, head_size)
    grad_qkv = lax.dot_general(
        normed_flat, qkv_flat, (((0,), (0,)), ((), ())), preferred_element_type=jnp.float32
    )
    grad_out = lax.dot_general(
        live_dy.reshape(-1, model_width),
        attended_flat,
        (((0,), (0,)), ((), ())),
        preferred_element_type=jnp.float32,
    )
    shares = (
        lax.psum_scatter(grad_qkv, "dp", scatter_dimension=0, tiled=True),
        lax.psum_scatter(grad_out, "dp", scatter_dimension=0, tiled=True),
    )
    shares = lax.psum((shares[0], shares[1]), "rep")
    gain_whole = lax.psum(gain_total, ("dp", "rep"))
    owned_rows = w_qkv.shape[0]
    gain_start = lax.axis_index("dp") * owned_rows
    gain_owned = lax.dynamic_slice_in_dim(gain_whole, gain_start, owned_rows, 0)
    replicas = lax.axis_size("rep")
    return (shares[0] / replicas, shares[1] / replicas, gain_owned / replicas)


MESH = pl.DeviceIdType.MESH
LANES = 128
CORES = 2


def mm(left, right, dims):
    return lax.dot_general(left, right, (dims, ((), ())), preferred_element_type=jnp.float32)


def eye(size):
    return lax.broadcasted_iota(jnp.int32, (size, size), 0) == lax.broadcasted_iota(
        jnp.int32, (size, size), 1
    )


def to_column(row):
    return jnp.sum(jnp.where(eye(row.shape[1]), row, 0.0), axis=1, keepdims=True)


def to_row(column):
    return jnp.sum(jnp.where(eye(column.shape[0]), column, 0.0), axis=0, keepdims=True)


def fused(
    n,
    replicas,
    x_ref,
    dy_ref,
    doc_ref,
    valid_ref,
    wq_ref,
    wo_ref,
    gain_ref,
    gq_ref,
    go_ref,
    gg_ref,
    w_all,
    gain_all,
    x_all,
    dy_all,
    y_all,
    acc,
    rs_send,
    rs_recv,
    g_all,
    w_send_sem,
    w_recv_sem,
    s_send_sem,
    s_recv_sem,
    a_send_sem,
    a_recv_sem,
    y_send_sem,
    y_recv_sem,
    r_send_sem,
    r_recv_sem,
    g_send_sem,
    g_recv_sem,
):
    me = lax.axis_index("dp")
    rep = lax.axis_index("rep")
    chip, core = me // CORES, lax.rem(me, CORES)
    sibling = chip * CORES + (1 - core)
    rows, width = x_ref.shape
    owned = wq_ref.shape[0]
    head = wo_ref.shape[1]
    wide = 3 * head
    samples, seq = doc_ref.shape
    piece = owned // replicas
    scale = 1.0 / math.sqrt(head)

    barrier = pltpu.get_barrier_semaphore()
    for off in range(1, n):
        pl.semaphore_signal(
            barrier, inc=1, device_id={"dp": lax.rem(me + off, n)}, device_id_type=MESH
        )
    for off in range(1, replicas):
        pl.semaphore_signal(
            barrier,
            inc=1,
            device_id={"rep": lax.rem(rep + off, replicas)},
            device_id_type=MESH,
        )

    gain_row = gain_ref[...].astype(jnp.float32)
    gain_col = to_column(gain_row)
    gain_all[me] = jnp.broadcast_to(gain_row, gain_all.shape[1:])
    my_w = pl.ds(pl.multiple_of(me * owned, LANES), owned)
    w_all[my_w, :wide] = wq_ref[...]
    w_all[my_w, wide:] = wo_ref[...]

    pl.semaphore_wait(barrier, n - 1 + replicas - 1)

    pending = []

    def send(src, dst, send_sem, recv_sem, where):
        copy = pltpu.make_async_remote_copy(
            src_ref=src,
            dst_ref=dst,
            send_sem=send_sem,
            recv_sem=recv_sem,
            device_id=where,
            device_id_type=MESH,
        )
        copy.start()
        pending.append(copy)
        return copy

    along, across = lax.rem(chip, 2), chip // 2
    by_x = across * 2 + 1 - along
    by_y = (1 - across) * 2 + along
    first = by_x + core * (by_y - by_x)
    second = by_y + core * (by_x - by_y)
    far = 3 - chip
    owners = (
        first * CORES + core,
        second * CORES + core,
        far * CORES + core,
        sibling,
        second * CORES + 1 - core,
        first * CORES + 1 - core,
        far * CORES + 1 - core,
    )

    def spread(buf, block, send_sem, recv_sem):
        def part(slot):
            start = pl.multiple_of(owners[slot] * block, LANES)
            return buf.at[pl.ds(start, block)]

        def copy(source, slot, device):
            return send(
                source, source, send_sem.at[slot], recv_sem.at[slot], {"dp": device}
            )

        mine = buf.at[pl.ds(pl.multiple_of(me * block, LANES), block)]
        straight = copy(mine, 0, owners[0])
        straight_second = copy(mine, 1, owners[1])
        passed = copy(mine, 3, sibling)
        yield None
        passed.wait_recv()
        yield owners[3]
        straight.wait_recv()
        relayed = copy(part(0), 2, owners[1])
        passed_first = copy(part(0), 4, sibling)
        yield owners[0]
        straight_second.wait_recv()
        passed_second = copy(part(1), 5, sibling)
        yield owners[1]
        passed_first.wait_recv()
        yield owners[4]
        passed_second.wait_recv()
        yield owners[5]
        relayed.wait_recv()
        passed_far = copy(part(2), 6, sibling)
        yield owners[2]
        passed_far.wait_recv()
        yield owners[6]

    arrivals = spread(w_all, owned, w_send_sem, w_recv_sem)
    next(arrivals)
    gains = {}
    for off in range(1, n):
        gains[off] = send(
            gain_all.at[me],
            gain_all.at[me],
            s_send_sem.at[off],
            s_recv_sem.at[off],
            {"dp": lax.rem(me + off, n)},
        )

    wide_in = x_ref[...].astype(jnp.float32)
    inverse = lax.rsqrt(
        jnp.sum(wide_in * wide_in, axis=1, keepdims=True) * (1.0 / width) + NORM_EPS
    )
    keys, live = [], []
    for m in range(samples):
        doc_row = doc_ref[m : m + 1, :].astype(jnp.float32)
        keys.append(to_column(doc_row) + float(m * seq))
        place = lax.broadcasted_iota(jnp.int32, (seq, 1), 0)
        live.append(jnp.where(place < valid_ref[m], 1.0, 0.0))
    key_col = jnp.concatenate(keys, axis=0)
    live_col = jnp.concatenate(live, axis=0)
    key_row = to_row(key_col)
    earlier = jnp.sum(jnp.where(key_row < key_col, 1.0, 0.0), axis=1, keepdims=True)
    order_row = lax.broadcasted_iota(jnp.int32, (rows, rows), 0)
    order_col = lax.broadcasted_iota(jnp.int32, (rows, rows), 1)
    allowed = (key_row == key_col) & (order_col <= order_row)
    offsets = lax.broadcasted_iota(jnp.int32, (rows, 1), 0).astype(jnp.float32) - earlier
    lane = lax.broadcasted_iota(jnp.int32, (1, head), 1)
    half = lax.rem(lane, head // 2).astype(jnp.float32)
    frequency = jnp.exp(half * (-2.0 / head * math.log(ROPE_BASE)))
    angles = offsets * frequency
    cosine = jnp.cos(angles)
    signed = jnp.sin(angles) * jnp.where(lane < head // 2, -1.0, 1.0)

    def times(source, total):
        cols = pl.ds(pl.multiple_of(source * owned, LANES), owned)
        scaled = x_ref[:, cols].astype(jnp.float32) * inverse
        normed = (scaled * gain_all[source][0:1]).astype(jnp.bfloat16)
        projected = mm(normed, w_all[cols, :wide], ((1,), (0,)))
        d_att = mm(dy_ref[:, cols], w_all[cols, wide:], ((1,), (0,)))
        if total is None:
            return projected, d_att
        return total[0] + projected, total[1] + d_att

    total = times(me, None)
    for off in range(1, n):
        gains[off].wait_recv()
    for source in itertools.islice(arrivals, n - 2):
        total = times(source, total)

    my_rows = pl.ds(pl.multiple_of(me * rows, LANES), rows)
    columns = {}
    for off in range(1, n):
        peer = lax.rem(me + off, n)
        cols = pl.ds(pl.multiple_of(peer * owned, LANES), owned)
        columns[off] = (
            send(
                x_ref.at[:, cols],
                x_all.at[my_rows],
                a_send_sem.at[0, off],
                a_recv_sem.at[0, off],
                {"dp": peer},
            ),
            send(
                dy_ref.at[:, cols],
                dy_all.at[my_rows],
                a_send_sem.at[1, off],
                a_recv_sem.at[1, off],
                {"dp": peer},
            ),
        )

    for source in arrivals:
        total = times(source, total)

    projected = total[0]
    d_att = (total[1] * live_col).astype(jnp.bfloat16)

    def turn(vector, sine_part):
        return vector * cosine + pltpu.roll(vector, head // 2, 1) * sine_part

    query = (turn(projected[:, :head], signed) * scale).astype(jnp.bfloat16)
    key = turn(projected[:, head : 2 * head], signed).astype(jnp.bfloat16)
    values = projected[:, 2 * head :].astype(jnp.bfloat16)
    scores = mm(query, key, ((1,), (1,)))
    raised = jnp.where(allowed, jnp.exp(scores), 0.0)
    probs = raised / jnp.sum(raised, axis=1, keepdims=True)
    probs_low = probs.astype(jnp.bfloat16)
    attended = mm(probs_low, values, ((1,), (0,)))
    d_probs = mm(d_att, values, ((1,), (1,)))
    d_values = mm(probs_low, d_att, ((0,), (0,)))
    d_scores = (
        probs * (d_probs - jnp.sum(probs * d_probs, axis=1, keepdims=True))
    ).astype(jnp.bfloat16)
    d_query = turn(mm(d_scores, key, ((1,), (0,))) * scale, -signed)
    d_key = turn(mm(d_scores, query, ((0,), (0,))), -signed)
    y_all[my_rows, :head] = (d_query * inverse).astype(jnp.bfloat16)
    y_all[my_rows, head : 2 * head] = (d_key * inverse).astype(jnp.bfloat16)
    y_all[my_rows, 2 * head : wide] = (d_values * inverse).astype(jnp.bfloat16)
    y_all[my_rows, wide:] = (attended * live_col).astype(jnp.bfloat16)

    arrivals = spread(y_all, rows, y_send_sem, y_recv_sem)
    next(arrivals)

    my_cols = pl.ds(pl.multiple_of(me * owned, LANES), owned)
    acc[:, :wide] = mm(x_ref[:, my_cols], y_all[my_rows, :wide], ((0,), (0,)))
    acc[:, wide:] = mm(dy_ref[:, my_cols], y_all[my_rows, wide:], ((0,), (0,)))
    for off in range(1, n):
        for copy in columns[off]:
            copy.wait_recv()

    def gather(source):
        part = pl.ds(pl.multiple_of(source * rows, LANES), rows)
        acc[:, :wide] += mm(x_all[part, :], y_all[part, :wide], ((0,), (0,)))
        acc[:, wide:] += mm(dy_all[part, :], y_all[part, wide:], ((0,), (0,)))

    for source in arrivals:
        gather(source)

    rs_send[...] = acc[...].astype(jnp.bfloat16)
    sums = []
    for off in range(1, replicas):
        peer = lax.rem(rep + off, replicas)
        part = pl.ds(pl.multiple_of(peer * piece, 16), piece)
        sums.append(
            send(
                rs_send.at[part],
                rs_recv.at[off - 1],
                r_send_sem.at[off],
                r_recv_sem.at[off],
                {"rep": peer},
            )
        )
    mine = pl.ds(pl.multiple_of(rep * piece, 16), piece)
    whole = acc[mine, :]
    for off in range(1, replicas):
        sums[off - 1].wait_recv()
        whole = whole + rs_recv[off - 1].astype(jnp.float32)
    g_all[mine, :] = (whole * (1.0 / replicas)).astype(jnp.bfloat16)
    last = []
    for off in range(1, replicas):
        peer = lax.rem(rep + off, replicas)
        last.append(
            send(
                g_all.at[mine],
                g_all.at[mine],
                g_send_sem.at[off],
                g_recv_sem.at[off],
                {"rep": peer},
            )
        )
    for copy in last:
        copy.wait_recv()
    total_q = g_all[:, :wide].astype(jnp.float32)
    gq_ref[...] = total_q * gain_col
    go_ref[...] = g_all[:, wide:].astype(jnp.float32)
    gg_ref[...] = to_row(
        jnp.sum(total_q * wq_ref[...].astype(jnp.float32), axis=1, keepdims=True)
    )
    for copy in pending:
        copy.wait_send()


def one_kernel(n, replicas, tokens, cotangent, doc_ids, valid_len, w_qkv, w_out, norm_gain):
    rows, width = tokens.shape
    owned, wide = w_qkv.shape
    head = w_out.shape[1]
    vmem = pl.BlockSpec(memory_space=pltpu.VMEM)
    smem = pl.BlockSpec(memory_space=pltpu.SMEM)
    low = jnp.bfloat16
    full = wide + head
    sem = pltpu.SemaphoreType.DMA
    grad_qkv, grad_out, grad_gain = pl.pallas_call(
        functools.partial(fused, n, replicas),
        out_shape=(
            jax.ShapeDtypeStruct((owned, wide), jnp.float32),
            jax.ShapeDtypeStruct((owned, head), jnp.float32),
            jax.ShapeDtypeStruct((1, owned), jnp.float32),
        ),
        in_specs=[vmem, vmem, vmem, smem, vmem, vmem, vmem],
        out_specs=(vmem, vmem, vmem),
        scratch_shapes=[
            pltpu.VMEM((width, full), low),
            pltpu.VMEM((n, 8, owned), jnp.float32),
            pltpu.VMEM((n * rows, owned), low),
            pltpu.VMEM((n * rows, owned), low),
            pltpu.VMEM((n * rows, full), low),
            pltpu.VMEM((owned, full), jnp.float32),
            pltpu.VMEM((owned, full), low),
            pltpu.VMEM((replicas - 1, owned // replicas, full), low),
            pltpu.VMEM((owned, full), low),
            sem((n - 1,)),
            sem((n - 1,)),
            sem((n,)),
            sem((n,)),
            sem((2, n)),
            sem((2, n)),
            sem((n - 1,)),
            sem((n - 1,)),
            sem((replicas,)),
            sem((replicas,)),
            sem((replicas,)),
            sem((replicas,)),
        ],
        compiler_params=pltpu.CompilerParams(
            collective_id=0, has_side_effects=True, vmem_limit_bytes=48 * 1024 * 1024
        ),
    )(tokens, cotangent, doc_ids, valid_len, w_qkv, w_out, norm_gain.reshape(1, owned))
    return grad_qkv, grad_out, grad_gain.reshape(owned)


def shards_or_kernel(
    n, replicas, tokens, cotangent, doc_ids, valid_len, w_qkv, w_out, norm_gain
):
    rows, owned, head = tokens.shape[0], w_qkv.shape[0], w_out.shape[1]
    fits = (
        n == 4 * CORES
        and replicas > 1
        and owned % LANES == 0
        and owned % (16 * replicas) == 0
        and rows % LANES == 0
        and rows * n <= 2048
        and head == LANES
        and doc_ids.shape[1] % 8 == 0
    )
    if not fits:
        return shards(tokens, cotangent, doc_ids, valid_len, w_qkv, w_out, norm_gain)
    return one_kernel(
        n, replicas, tokens, cotangent, doc_ids, valid_len, w_qkv, w_out, norm_gain
    )


def solution(mesh):
    in_specs = (
        P(("dp", "rep"), None),
        P(("dp", "rep"), None),
        P(("dp", "rep"), None),
        P(("dp", "rep")),
        P("dp", None),
        P("dp", None),
        P("dp"),
    )
    out_specs = (P("dp", None), P("dp", None), P("dp"))
    body = functools.partial(shards_or_kernel, mesh.shape["dp"], mesh.shape["rep"])
    return jax.shard_map(body, mesh=mesh, in_specs=in_specs, out_specs=out_specs, check_vma=False)
```

```python
import functools
import itertools
import math

import jax
import jax.numpy as jnp
from jax import lax
from jax.experimental import pallas as pl
from jax.experimental.pallas import tpu as pltpu
from jax.sharding import PartitionSpec as P

NORM_EPS = 1e-06
ROPE_BASE = 1000000.0


def rotate(vector):
    half_size = vector.shape[-1] // 2
    return jnp.concatenate([-vector[..., half_size:], vector[..., :half_size]], axis=-1)


def unrotate(vector):
    half_size = vector.shape[-1] // 2
    return jnp.concatenate([vector[..., half_size:], -vector[..., :half_size]], axis=-1)


def tables(doc_rows, head_size):
    seq_length = doc_rows.shape[1]
    earlier = jnp.sum((doc_rows[:, None, :] < doc_rows[:, :, None]).astype(jnp.int32), axis=2)
    offsets = (jnp.arange(seq_length, dtype=jnp.int32)[None, :] - earlier).astype(jnp.float32)
    frequency = ROPE_BASE ** (-2.0 * jnp.arange(head_size // 2, dtype=jnp.float32) / head_size)
    angles = offsets[:, :, None] * frequency
    angles = jnp.concatenate([angles, angles], axis=2)
    return (jnp.cos(angles), jnp.sin(angles))


def forward_pass(inputs, doc_rows, w_qkv_full, gain_full):
    batches, seq_length, model_width = inputs.shape
    head_size = w_qkv_full.shape[1] // 3
    scale = 1.0 / math.sqrt(head_size)
    wide_in = inputs.astype(jnp.float32)
    inverse_rms = lax.rsqrt(jnp.mean(wide_in * wide_in, axis=2, keepdims=True) + NORM_EPS)
    scaled_in = wide_in * inverse_rms
    normed = (scaled_in * gain_full.astype(jnp.float32)).astype(jnp.bfloat16)
    projected = jnp.dot(
        normed.reshape(-1, model_width), w_qkv_full, preferred_element_type=jnp.float32
    )
    projected = projected.reshape(batches, seq_length, 3 * head_size)
    cosine, sine_part = tables(doc_rows, head_size)
    queries = projected[:, :, :head_size]
    keys_raw = projected[:, :, head_size : 2 * head_size]
    values_raw = projected[:, :, 2 * head_size :]
    query_rot = ((queries * cosine + rotate(queries) * sine_part) * scale).astype(jnp.bfloat16)
    key_rot = (keys_raw * cosine + rotate(keys_raw) * sine_part).astype(jnp.bfloat16)
    values = values_raw.astype(jnp.bfloat16)
    scores = jnp.einsum("msh,mth->mst", query_rot, key_rot, preferred_element_type=jnp.float32)
    order_row = jnp.arange(seq_length, dtype=jnp.int32)[:, None]
    order_col = jnp.arange(seq_length, dtype=jnp.int32)[None, :]
    allowed = (doc_rows[:, :, None] == doc_rows[:, None, :]) & (order_col <= order_row)[None]
    raised = jnp.where(allowed, jnp.exp(scores), 0.0)
    probabilities = raised / jnp.sum(raised, axis=2, keepdims=True)
    probs_low = probabilities.astype(jnp.bfloat16)
    attended = jnp.einsum(
        "mst,mth->msh", probs_low, values, preferred_element_type=jnp.float32
    ).astype(jnp.bfloat16)
    return (
        scaled_in,
        normed,
        query_rot,
        key_rot,
        values,
        probabilities,
        probs_low,
        attended,
        cosine,
        sine_part,
    )


def backward_pass(saved, live_dy, w_qkv_full, w_out_full):
    (
        scaled_in,
        normed,
        query_rot,
        key_rot,
        values,
        probabilities,
        probs_low,
        attended,
        cosine,
        sine_part,
    ) = saved
    batches, seq_length, model_width = live_dy.shape
    head_size = w_out_full.shape[1]
    scale = 1.0 / math.sqrt(head_size)
    d_attended = jnp.dot(
        live_dy.reshape(-1, model_width), w_out_full, preferred_element_type=jnp.float32
    )
    d_attended = d_attended.reshape(batches, seq_length, head_size).astype(jnp.bfloat16)
    d_probs = jnp.einsum("msh,mth->mst", d_attended, values, preferred_element_type=jnp.float32)
    d_values = jnp.einsum("mst,msh->mth", probs_low, d_attended, preferred_element_type=jnp.float32)
    d_scores = (
        probabilities * (d_probs - jnp.sum(probabilities * d_probs, axis=2, keepdims=True))
    ).astype(jnp.bfloat16)
    d_query = (
        jnp.einsum("mst,mth->msh", d_scores, key_rot, preferred_element_type=jnp.float32) * scale
    )
    d_key = jnp.einsum("mst,msh->mth", d_scores, query_rot, preferred_element_type=jnp.float32)
    d_query = d_query * cosine + unrotate(d_query * sine_part)
    d_key = d_key * cosine + unrotate(d_key * sine_part)
    d_qkv = jnp.concatenate([d_query, d_key, d_values], axis=2).astype(jnp.bfloat16)
    d_normed = lax.dot_general(
        d_qkv.reshape(-1, 3 * head_size),
        w_qkv_full,
        (((1,), (1,)), ((), ())),
        preferred_element_type=jnp.float32,
    )
    gain_term = jnp.sum(d_normed * scaled_in.reshape(-1, model_width), axis=0)
    return (d_qkv, gain_term)


def shards(tokens, cotangent, doc_ids, valid_len, w_qkv, w_out, norm_gain):
    batches, seq_length = doc_ids.shape
    model_width = tokens.shape[1]
    inputs = tokens.reshape(batches, seq_length, model_width)
    live_rows = jnp.arange(seq_length, dtype=jnp.int32)[None, :] < valid_len[:, None]
    live_dy = jnp.where(
        live_rows[:, :, None],
        cotangent.reshape(batches, seq_length, model_width),
        jnp.zeros((), jnp.bfloat16),
    )
    full_set = (
        lax.all_gather(w_qkv, "dp", axis=0, tiled=True),
        lax.all_gather(w_out, "dp", axis=0, tiled=True),
        lax.all_gather(norm_gain, "dp", axis=0, tiled=True),
    )
    saved = forward_pass(inputs, doc_ids, full_set[0], full_set[2])
    qkv_all, gain_total = backward_pass(saved, live_dy, full_set[0], full_set[1])
    normed_all = saved[1]
    attended_all = saved[7]
    head_size = w_out.shape[1]
    normed_flat = normed_all.reshape(-1, model_width)
    qkv_flat = qkv_all.reshape(-1, 3 * head_size)
    attended_flat = attended_all.reshape(-1, head_size)
    grad_qkv = lax.dot_general(
        normed_flat, qkv_flat, (((0,), (0,)), ((), ())), preferred_element_type=jnp.float32
    )
    grad_out = lax.dot_general(
        live_dy.reshape(-1, model_width),
        attended_flat,
        (((0,), (0,)), ((), ())),
        preferred_element_type=jnp.float32,
    )
    shares = (
        lax.psum_scatter(grad_qkv, "dp", scatter_dimension=0, tiled=True),
        lax.psum_scatter(grad_out, "dp", scatter_dimension=0, tiled=True),
    )
    shares = lax.psum((shares[0], shares[1]), "rep")
    gain_whole = lax.psum(gain_total, ("dp", "rep"))
    owned_rows = w_qkv.shape[0]
    gain_start = lax.axis_index("dp") * owned_rows
    gain_owned = lax.dynamic_slice_in_dim(gain_whole, gain_start, owned_rows, 0)
    replicas = lax.axis_size("rep")
    return (shares[0] / replicas, shares[1] / replicas, gain_owned / replicas)


MESH = pl.DeviceIdType.MESH
LANES = 128
CORES = 2


def mm(left, right, dims):
    return lax.dot_general(left, right, (dims, ((), ())), preferred_element_type=jnp.float32)


def eye(size):
    return lax.broadcasted_iota(jnp.int32, (size, size), 0) == lax.broadcasted_iota(
        jnp.int32, (size, size), 1
    )


def to_column(row):
    return jnp.sum(jnp.where(eye(row.shape[1]), row, 0.0), axis=1, keepdims=True)


def to_row(column):
    return jnp.sum(jnp.where(eye(column.shape[0]), column, 0.0), axis=0, keepdims=True)


def fused(
    n,
    replicas,
    x_hbm,
    dy_hbm,
    doc_ref,
    valid_ref,
    wq_hbm,
    wo_hbm,
    gain_ref,
    gq_ref,
    go_ref,
    gg_ref,
    x_ref,
    dy_ref,
    in_sem,
    w_all,
    gain_all,
    x_all,
    dy_all,
    y_all,
    acc,
    rs_send,
    rs_recv,
    g_all,
    w_send_sem,
    w_recv_sem,
    s_send_sem,
    s_recv_sem,
    a_send_sem,
    a_recv_sem,
    y_send_sem,
    y_recv_sem,
    r_send_sem,
    r_recv_sem,
    g_send_sem,
    g_recv_sem,
):
    me = lax.axis_index("dp")
    rep = lax.axis_index("rep")
    chip, core = me // CORES, lax.rem(me, CORES)
    sibling = chip * CORES + (1 - core)
    rows, width = x_ref.shape
    owned = wq_hbm.shape[0]
    head = wo_hbm.shape[1]
    wide = 3 * head
    samples, seq = doc_ref.shape
    piece = owned // replicas
    scale = 1.0 / math.sqrt(head)

    my_w = pl.ds(pl.multiple_of(me * owned, LANES), owned)
    loads = (
        pltpu.make_async_copy(wq_hbm, w_all.at[my_w, pl.ds(0, wide)], in_sem.at[0]),
        pltpu.make_async_copy(wo_hbm, w_all.at[my_w, pl.ds(wide, head)], in_sem.at[1]),
        pltpu.make_async_copy(x_hbm, x_ref, in_sem.at[2]),
        pltpu.make_async_copy(dy_hbm, dy_ref, in_sem.at[3]),
    )
    for load in loads:
        load.start()

    barrier = pltpu.get_barrier_semaphore()
    for off in range(1, n):
        pl.semaphore_signal(
            barrier, inc=1, device_id={"dp": lax.rem(me + off, n)}, device_id_type=MESH
        )
    for off in range(1, replicas):
        pl.semaphore_signal(
            barrier,
            inc=1,
            device_id={"rep": lax.rem(rep + off, replicas)},
            device_id_type=MESH,
        )

    gain_row = gain_ref[...].astype(jnp.float32)
    gain_col = to_column(gain_row)
    gain_all[me] = jnp.broadcast_to(gain_row, gain_all.shape[1:])
    loads[0].wait()
    loads[1].wait()
    pl.semaphore_wait(barrier, n - 1 + replicas - 1)

    pending = []

    def send(src, dst, send_sem, recv_sem, where):
        copy = pltpu.make_async_remote_copy(
            src_ref=src,
            dst_ref=dst,
            send_sem=send_sem,
            recv_sem=recv_sem,
            device_id=where,
            device_id_type=MESH,
        )
        copy.start()
        pending.append(copy)
        return copy

    along, across = lax.rem(chip, 2), chip // 2
    by_x = across * 2 + 1 - along
    by_y = (1 - across) * 2 + along
    first = by_x + core * (by_y - by_x)
    second = by_y + core * (by_x - by_y)
    far = 3 - chip
    owners = (
        first * CORES + core,
        second * CORES + core,
        far * CORES + core,
        sibling,
        second * CORES + 1 - core,
        first * CORES + 1 - core,
        far * CORES + 1 - core,
    )

    def spread(buf, block, send_sem, recv_sem):
        def part(slot):
            start = pl.multiple_of(owners[slot] * block, LANES)
            return buf.at[pl.ds(start, block)]

        def copy(source, slot, device):
            return send(
                source, source, send_sem.at[slot], recv_sem.at[slot], {"dp": device}
            )

        mine = buf.at[pl.ds(pl.multiple_of(me * block, LANES), block)]
        straight = copy(mine, 0, owners[0])
        straight_second = copy(mine, 1, owners[1])
        passed = copy(mine, 3, sibling)
        yield None
        passed.wait_recv()
        yield owners[3]
        straight.wait_recv()
        relayed = copy(part(0), 2, owners[1])
        passed_first = copy(part(0), 4, sibling)
        yield owners[0]
        straight_second.wait_recv()
        passed_second = copy(part(1), 5, sibling)
        yield owners[1]
        passed_first.wait_recv()
        yield owners[4]
        passed_second.wait_recv()
        yield owners[5]
        relayed.wait_recv()
        passed_far = copy(part(2), 6, sibling)
        yield owners[2]
        passed_far.wait_recv()
        yield owners[6]

    arrivals = spread(w_all, owned, w_send_sem, w_recv_sem)
    next(arrivals)
    gains = {}
    for off in range(1, n):
        gains[off] = send(
            gain_all.at[me],
            gain_all.at[me],
            s_send_sem.at[off],
            s_recv_sem.at[off],
            {"dp": lax.rem(me + off, n)},
        )

    loads[2].wait()
    loads[3].wait()
    wide_in = x_ref[...].astype(jnp.float32)
    inverse = lax.rsqrt(
        jnp.sum(wide_in * wide_in, axis=1, keepdims=True) * (1.0 / width) + NORM_EPS
    )
    keys, live = [], []
    for m in range(samples):
        doc_row = doc_ref[m : m + 1, :].astype(jnp.float32)
        keys.append(to_column(doc_row) + float(m * seq))
        place = lax.broadcasted_iota(jnp.int32, (seq, 1), 0)
        live.append(jnp.where(place < valid_ref[m], 1.0, 0.0))
    key_col = jnp.concatenate(keys, axis=0)
    live_col = jnp.concatenate(live, axis=0)
    key_row = to_row(key_col)
    earlier = jnp.sum(jnp.where(key_row < key_col, 1.0, 0.0), axis=1, keepdims=True)
    order_row = lax.broadcasted_iota(jnp.int32, (rows, rows), 0)
    order_col = lax.broadcasted_iota(jnp.int32, (rows, rows), 1)
    allowed = (key_row == key_col) & (order_col <= order_row)
    offsets = lax.broadcasted_iota(jnp.int32, (rows, 1), 0).astype(jnp.float32) - earlier
    lane = lax.broadcasted_iota(jnp.int32, (1, head), 1)
    half = lax.rem(lane, head // 2).astype(jnp.float32)
    frequency = jnp.exp(half * (-2.0 / head * math.log(ROPE_BASE)))
    angles = offsets * frequency
    cosine = jnp.cos(angles)
    signed = jnp.sin(angles) * jnp.where(lane < head // 2, -1.0, 1.0)

    def times(source, total):
        cols = pl.ds(pl.multiple_of(source * owned, LANES), owned)
        scaled = x_ref[:, cols].astype(jnp.float32) * inverse
        normed = (scaled * gain_all[source][0:1]).astype(jnp.bfloat16)
        projected = mm(normed, w_all[cols, :wide], ((1,), (0,)))
        d_att = mm(dy_ref[:, cols], w_all[cols, wide:], ((1,), (0,)))
        if total is None:
            return projected, d_att
        return total[0] + projected, total[1] + d_att

    total = times(me, None)
    for off in range(1, n):
        gains[off].wait_recv()
    for source in itertools.islice(arrivals, n - 2):
        total = times(source, total)

    my_rows = pl.ds(pl.multiple_of(me * rows, LANES), rows)
    columns = {}
    for off in range(1, n):
        peer = lax.rem(me + off, n)
        cols = pl.ds(pl.multiple_of(peer * owned, LANES), owned)
        columns[off] = (
            send(
                x_ref.at[:, cols],
                x_all.at[my_rows],
                a_send_sem.at[0, off],
                a_recv_sem.at[0, off],
                {"dp": peer},
            ),
            send(
                dy_ref.at[:, cols],
                dy_all.at[my_rows],
                a_send_sem.at[1, off],
                a_recv_sem.at[1, off],
                {"dp": peer},
            ),
        )

    for source in arrivals:
        total = times(source, total)

    projected = total[0]
    d_att = (total[1] * live_col).astype(jnp.bfloat16)

    def turn(vector, sine_part):
        return vector * cosine + pltpu.roll(vector, head // 2, 1) * sine_part

    query = (turn(projected[:, :head], signed) * scale).astype(jnp.bfloat16)
    key = turn(projected[:, head : 2 * head], signed).astype(jnp.bfloat16)
    values = projected[:, 2 * head :].astype(jnp.bfloat16)
    scores = mm(query, key, ((1,), (1,)))
    raised = jnp.where(allowed, jnp.exp(scores), 0.0)
    probs = raised / jnp.sum(raised, axis=1, keepdims=True)
    probs_low = probs.astype(jnp.bfloat16)
    attended = mm(probs_low, values, ((1,), (0,)))
    d_probs = mm(d_att, values, ((1,), (1,)))
    d_values = mm(probs_low, d_att, ((0,), (0,)))
    d_scores = (
        probs * (d_probs - jnp.sum(probs * d_probs, axis=1, keepdims=True))
    ).astype(jnp.bfloat16)
    d_query = turn(mm(d_scores, key, ((1,), (0,))) * scale, -signed)
    d_key = turn(mm(d_scores, query, ((0,), (0,))), -signed)
    y_all[my_rows, :head] = (d_query * inverse).astype(jnp.bfloat16)
    y_all[my_rows, head : 2 * head] = (d_key * inverse).astype(jnp.bfloat16)
    y_all[my_rows, 2 * head : wide] = (d_values * inverse).astype(jnp.bfloat16)
    y_all[my_rows, wide:] = (attended * live_col).astype(jnp.bfloat16)

    arrivals = spread(y_all, rows, y_send_sem, y_recv_sem)
    next(arrivals)

    my_cols = pl.ds(pl.multiple_of(me * owned, LANES), owned)
    acc[:, :wide] = mm(x_ref[:, my_cols], y_all[my_rows, :wide], ((0,), (0,)))
    acc[:, wide:] = mm(dy_ref[:, my_cols], y_all[my_rows, wide:], ((0,), (0,)))
    for off in range(1, n):
        for copy in columns[off]:
            copy.wait_recv()

    def gather(source):
        part = pl.ds(pl.multiple_of(source * rows, LANES), rows)
        acc[:, :wide] += mm(x_all[part, :], y_all[part, :wide], ((0,), (0,)))
        acc[:, wide:] += mm(dy_all[part, :], y_all[part, wide:], ((0,), (0,)))

    for source in arrivals:
        gather(source)

    rs_send[...] = acc[...].astype(jnp.bfloat16)
    sums = []
    for off in range(1, replicas):
        peer = lax.rem(rep + off, replicas)
        part = pl.ds(pl.multiple_of(peer * piece, 16), piece)
        sums.append(
            send(
                rs_send.at[part],
                rs_recv.at[off - 1],
                r_send_sem.at[off],
                r_recv_sem.at[off],
                {"rep": peer},
            )
        )
    mine = pl.ds(pl.multiple_of(rep * piece, 16), piece)
    whole = acc[mine, :]
    for off in range(1, replicas):
        sums[off - 1].wait_recv()
        whole = whole + rs_recv[off - 1].astype(jnp.float32)
    g_all[mine, :] = (whole * (1.0 / replicas)).astype(jnp.bfloat16)
    last = []
    for off in range(1, replicas):
        peer = lax.rem(rep + off, replicas)
        last.append(
            send(
                g_all.at[mine],
                g_all.at[mine],
                g_send_sem.at[off],
                g_recv_sem.at[off],
                {"rep": peer},
            )
        )
    for copy in last:
        copy.wait_recv()
    total_q = g_all[:, :wide].astype(jnp.float32)
    gq_ref[...] = total_q * gain_col
    go_ref[...] = g_all[:, wide:].astype(jnp.float32)
    gg_ref[...] = to_row(
        jnp.sum(total_q * w_all[my_w, :wide].astype(jnp.float32), axis=1, keepdims=True)
    )
    for copy in pending:
        copy.wait_send()


def one_kernel(n, replicas, tokens, cotangent, doc_ids, valid_len, w_qkv, w_out, norm_gain):
    rows, width = tokens.shape
    owned, wide = w_qkv.shape
    head = w_out.shape[1]
    vmem = pl.BlockSpec(memory_space=pltpu.VMEM)
    hbm = pl.BlockSpec(memory_space=pltpu.HBM)
    smem = pl.BlockSpec(memory_space=pltpu.SMEM)
    low = jnp.bfloat16
    full = wide + head
    sem = pltpu.SemaphoreType.DMA
    grad_qkv, grad_out, grad_gain = pl.pallas_call(
        functools.partial(fused, n, replicas),
        out_shape=(
            jax.ShapeDtypeStruct((owned, wide), jnp.float32),
            jax.ShapeDtypeStruct((owned, head), jnp.float32),
            jax.ShapeDtypeStruct((1, owned), jnp.float32),
        ),
        in_specs=[hbm, hbm, vmem, smem, hbm, hbm, vmem],
        out_specs=(vmem, vmem, vmem),
        scratch_shapes=[
            pltpu.VMEM((rows, width), low),
            pltpu.VMEM((rows, width), low),
            sem((4,)),
            pltpu.VMEM((width, full), low),
            pltpu.VMEM((n, 8, owned), jnp.float32),
            pltpu.VMEM((n * rows, owned), low),
            pltpu.VMEM((n * rows, owned), low),
            pltpu.VMEM((n * rows, full), low),
            pltpu.VMEM((owned, full), jnp.float32),
            pltpu.VMEM((owned, full), low),
            pltpu.VMEM((replicas - 1, owned // replicas, full), low),
            pltpu.VMEM((owned, full), low),
            sem((n - 1,)),
            sem((n - 1,)),
            sem((n,)),
            sem((n,)),
            sem((2, n)),
            sem((2, n)),
            sem((n - 1,)),
            sem((n - 1,)),
            sem((replicas,)),
            sem((replicas,)),
            sem((replicas,)),
            sem((replicas,)),
        ],
        compiler_params=pltpu.CompilerParams(
            collective_id=0, has_side_effects=True, vmem_limit_bytes=48 * 1024 * 1024
        ),
    )(tokens, cotangent, doc_ids, valid_len, w_qkv, w_out, norm_gain.reshape(1, owned))
    return grad_qkv, grad_out, grad_gain.reshape(owned)


def shards_or_kernel(
    n, replicas, tokens, cotangent, doc_ids, valid_len, w_qkv, w_out, norm_gain
):
    rows, owned, head = tokens.shape[0], w_qkv.shape[0], w_out.shape[1]
    fits = (
        n == 4 * CORES
        and replicas > 1
        and owned % LANES == 0
        and owned % (16 * replicas) == 0
        and rows % LANES == 0
        and rows * n <= 2048
        and head == LANES
        and doc_ids.shape[1] % 8 == 0
    )
    if not fits:
        return shards(tokens, cotangent, doc_ids, valid_len, w_qkv, w_out, norm_gain)
    return one_kernel(
        n, replicas, tokens, cotangent, doc_ids, valid_len, w_qkv, w_out, norm_gain
    )


def solution(mesh):
    in_specs = (
        P(("dp", "rep"), None),
        P(("dp", "rep"), None),
        P(("dp", "rep"), None),
        P(("dp", "rep")),
        P("dp", None),
        P("dp", None),
        P("dp"),
    )
    out_specs = (P("dp", None), P("dp", None), P("dp"))
    body = functools.partial(shards_or_kernel, mesh.shape["dp"], mesh.shape["rep"])
    return jax.shard_map(body, mesh=mesh, in_specs=in_specs, out_specs=out_specs, check_vma=False)
```
